32 devices in a mesh: groups: 2 (over y), blk: 16 (over z, x, core).
Axes of the slice: x: 2, y: 2, z: 4, core: 2. Of those that a mesh axis runs over, the one named last changes fastest.
Arguments:
- ensemble: bfloat16 [256, 131072], P(None, ('groups', 'blk')), parts along dimension 1, may hold values from -6 to 6
- predicted: bfloat16 [256, 4096], P(None, ('groups', 'blk')), parts along dimension 1, may hold values from -6 to 6
- targets: bfloat16 [256, 4096], P(None, ('groups', 'blk')), parts along dimension 1, may hold values from -9 to 9
- datum_noise_variance: float32 [4096], P(('groups', 'blk')), parts along dimension 0, may hold values from 0.16 to 2, as said below
- block_ids: int32 [32], P('groups'), parts along dimension 0, may hold values from 0 to 15, each once
- pair_blocks: int32 [512, 16], P(('groups', 'blk')), parts along dimension 0, may hold values from 0 to 15
- taper: float32 [512, 16], P(('groups', 'blk')), parts along dimension 0, may hold values from 0.2 to 1
Outputs:
- ensemble_step: float32 [256, 131072], P(None, ('groups', 'blk')), parts along dimension 1
The draws below stay inside these ranges and needn't reach their ends.
There are 2 independent parts, one for each index of `groups`. The reference program is written for one: setup_inputs(seed, part) draws one part's arguments, and reference() takes and returns one part's arrays. A program takes and returns all parts, laid end to end along the dimension named above; each array names one. Nothing has to cross between parts.
Inputs may be any that keep to these rules, and one draw needn't show every extreme that they name: `datum_noise_variance`: a variance that falls threefold from the first datum to the last, times an independent factor between 0.5 and 2, clipped to the range. `block_ids`: each data block is held in exactly one slot.
All inputs are finite; a program needn't handle non-finite values.
Results may differ from the reference program's by a relative error of at most 0.033.
Values may be sent and summed in bfloat16 or wider, within the bound.
A program may use at most 128 MiB of HBM per device.

```python
import math
import jax
import jax.numpy as jnp
from jax import lax

BLOCK = 256
DATA_PER_BLOCK = 128
MEM = 256
PAIRS = 16
BLOCK_COUNT = 16
NC = 256
CELLS = 65536
DATA = 2048


def shared_patterns(key):
    factor_count = 32
    pattern_key = jax.random.fold_in(key, 7331)
    base_key = jax.random.fold_in(key, 7919)
    weight_key = jax.random.fold_in(key, 8623)
    patterns = jax.random.normal(pattern_key, (factor_count, DATA), jnp.float32)
    base_field = 0.6 * jax.random.normal(base_key, (DATA,), jnp.float32)
    truth_weights = jax.random.normal(weight_key, (factor_count,), jnp.float32)
    strengths = 0.6 * jnp.exp(-math.log(100.0) * jnp.arange(factor_count, dtype=jnp.float32) / (factor_count - 1.0))
    return (patterns, base_field, truth_weights, strengths)


def draw_predicted(key, part):
    patterns, base_field, truth_weights, strengths = shared_patterns(key)
    factor_count = patterns.shape[0]
    member_key = jax.random.fold_in(key, 4409)
    noise_key = jax.random.fold_in(key, 5113)
    member_factors = jax.random.normal(member_key, (MEM, factor_count), jnp.float32)
    noise_values = jax.random.normal(noise_key, (MEM, DATA), jnp.float32)
    field = base_field[None, :] + 0.2 * noise_values
    for factor_index in range(factor_count):
        column = member_factors[:, factor_index:factor_index + 1] * strengths[factor_index]
        field = field + column * patterns[factor_index][None, :]
    return jnp.clip(field, -6.0, 6.0).astype(jnp.bfloat16)


def draw_targets(key, part):
    patterns, base_field, truth_weights, strengths = shared_patterns(key)
    factor_count = patterns.shape[0]
    perturb_key = jax.random.fold_in(key, 6271)
    perturbation = jax.random.normal(perturb_key, (MEM, DATA), jnp.float32)
    observed = base_field
    for factor_index in range(factor_count):
        observed = observed + truth_weights[factor_index] * strengths[factor_index] * patterns[factor_index]
    field = observed[None, :] + 0.7 * perturbation
    return jnp.clip(field, -9.0, 9.0).astype(jnp.bfloat16)


def draw_datum_noise_variance(key, part):
    position = jnp.arange(DATA, dtype=jnp.float32) / DATA
    ramp = jnp.exp(-jnp.log(3.0) * position)
    factor = jnp.exp(jax.random.uniform(key, (DATA,), jnp.float32, jnp.log(0.5), jnp.log(2.0)))
    return jnp.clip(ramp * factor, 0.16, 2.0).astype(jnp.float32)


def place_ends(array, rng, low, largest):
    longest = array.shape.index(max(array.shape))
    spots = []
    for shift in (0, 1):
        where = [jax.random.randint(jax.random.fold_in(rng, axis), (), 0, length) for axis, length in enumerate(array.shape)]
        where[longest] = (where[longest] + shift) % array.shape[longest]
        spots.append(tuple(where))
    return array.at[spots[0]].set(low).at[spots[1]].set(largest)


def steps_of(key, dims, cuts, low, largest):
    def one(axis_at, parts):
        steps = jax.random.uniform(jax.random.fold_in(jax.random.fold_in(key, 6), axis_at), (parts,), jnp.float32, low / len(cuts), largest / len(cuts))
        return jnp.repeat(jnp.exp(steps), dims[axis_at] // parts).reshape((-1,) + (1,) * (len(dims) - axis_at - 1))

    level = one(*cuts[0])
    for cut in cuts[1:]:
        level = level * one(*cut)
    return level


def gaussian(rng, dims, width, limit, pieces=(), held_as=jnp.bfloat16):
    level = steps_of(rng, dims, pieces, -0.22, 0.18) if pieces else 1.0
    entries = jax.random.normal(rng, dims, jnp.float32) * width * level
    return jnp.minimum(jnp.maximum(entries, -limit), limit).astype(held_as)


def setup_inputs(seed: int = 0, part: int = 0) -> dict:
    keys = jax.random.split(jax.random.key(seed), 8)
    own_keys = jax.random.split(jax.random.fold_in(keys[7], part), 8)
    ensemble = gaussian(own_keys[0], (MEM, CELLS), 1.0, 6.0, ((1, 16),))
    predicted = draw_predicted(jax.random.fold_in(jax.random.fold_in(keys[7], part), 71), part)
    targets = draw_targets(jax.random.fold_in(jax.random.fold_in(keys[7], part), 71), part)
    datum_noise_variance = draw_datum_noise_variance(jax.random.fold_in(jax.random.fold_in(keys[7], part), 71), part)
    block_ids = jax.random.permutation(own_keys[4], BLOCK_COUNT).astype(jnp.int32)
    pair_blocks = place_ends(jax.random.randint(own_keys[5], (NC, PAIRS), 0, BLOCK_COUNT), jax.random.fold_in(own_keys[5], 1), 0, BLOCK_COUNT - 1).astype(jnp.int32)
    taper = jnp.clip(0.2 + 0.8 * jax.random.uniform(own_keys[6], (NC, PAIRS), jnp.float32) ** steps_of(own_keys[6], (NC, PAIRS), ((0, 16),), -0.2, 0.2), 0.2, 1.0)
    return {"ensemble": ensemble, "predicted": predicted, "targets": targets, "datum_noise_variance": datum_noise_variance, "block_ids": block_ids, "pair_blocks": pair_blocks, "taper": taper}


def chol_solve(zmat, rhs):
    factor = jnp.linalg.cholesky(zmat)
    lower_part = lax.linalg.triangular_solve(factor, rhs, left_side=True, lower=True)
    return lax.linalg.triangular_solve(factor, lower_part, left_side=True, lower=True, transpose_a=True)

def reference(ensemble, predicted, targets, datum_noise_variance, block_ids, pair_blocks, taper):
    single_float = jnp.float32
    ensemble_members = ensemble.shape[0]
    uanom = (ensemble.astype(single_float) - jnp.mean(ensemble.astype(single_float), axis=0)).astype(jnp.bfloat16)
    data_deviation = (predicted.astype(single_float) - jnp.mean(predicted.astype(single_float), axis=0)).astype(jnp.bfloat16)
    resid_full = targets.astype(single_float) - predicted.astype(single_float)
    residual_misfit = resid_full.astype(jnp.bfloat16)
    scaled = (data_deviation.astype(single_float) / datum_noise_variance).astype(jnp.bfloat16)
    gram = jnp.dot(scaled, data_deviation.T, preferred_element_type=single_float)
    cross = jnp.dot(scaled, residual_misfit.T, preferred_element_type=single_float)
    zmat = gram + (ensemble_members - 1.0) * jnp.eye(ensemble_members, dtype=single_float)
    xmat = chol_solve(zmat, cross)
    update_term = jnp.dot(xmat.T, data_deviation.astype(single_float), precision=lax.Precision.HIGHEST)
    solved_matrix = ((residual_misfit.astype(single_float) - update_term) / datum_noise_variance).astype(jnp.bfloat16)
    dblocks = data_deviation.astype(single_float).reshape(ensemble_members, BLOCK_COUNT, DATA_PER_BLOCK)
    solved_blocks = solved_matrix.astype(single_float).reshape(ensemble_members, BLOCK_COUNT, DATA_PER_BLOCK)
    gains = (jnp.einsum('ikd,jkd->kij', dblocks, solved_blocks) / (ensemble_members - 1.0)).astype(jnp.bfloat16)
    flat_gains = gains.astype(single_float).reshape(BLOCK_COUNT, ensemble_members * ensemble_members)
    match = (pair_blocks[:, :, None] == block_ids[None, None, :]).astype(single_float)
    weight = jnp.sum(taper[:, :, None] * match, axis=1)
    ublocks = jnp.transpose(uanom.reshape(ensemble_members, NC, BLOCK), (1, 0, 2))

    def one_block(item):
        wrow, ublock = item
        gsum = jnp.dot(wrow, flat_gains, precision=lax.Precision.HIGHEST)
        gsum = gsum.reshape(ensemble_members, ensemble_members).astype(jnp.bfloat16)
        return jnp.dot(gsum.T, ublock, preferred_element_type=single_float)
    result = lax.map(one_block, (weight, ublocks))
    return jnp.transpose(result, (1, 0, 2)).reshape(ensemble_members, NC * BLOCK)
```

```python
import functools

import jax
import jax.numpy as jnp
from jax import lax
from jax.experimental import pallas as pl
from jax.experimental.pallas import tpu as pltpu
from jax.sharding import PartitionSpec as P

MESH = pl.DeviceIdType.MESH
F32 = jnp.float32
BF16 = jnp.bfloat16
HIGHEST = lax.Precision.HIGHEST
NT = (((1,), (1,)), ((), ()))
PANEL = 64


def chip_grid(n):
    chips = n // 2
    nx = max(f for f in range(1, chips + 1) if chips % f == 0 and f * f * f <= chips)
    return chips // nx, nx


def gather_kernel(
    nz, nx, pred, targ, var, dev, res, var_row, gram, cross,
    buf, vbuf, local_sem, send_sem, vsend_sem, recv_sem, vrecv_sem,
):
    width = buf.shape[-1]
    me = lax.axis_index("blk")
    core = me % 2
    x = (me // 2) % nx
    z = me // (2 * nx)
    exists = (z < nz - 1, z > 0, x < nx - 1, x > 0, core >= 0)
    target = (me + 2 * nx, me - 2 * nx, me + 2, me - 2, me + 1 - 2 * core)

    local = (
        pltpu.make_async_copy(pred, buf.at[me, 0], local_sem.at[0]),
        pltpu.make_async_copy(targ, buf.at[me, 1], local_sem.at[1]),
        pltpu.make_async_copy(var, vbuf.at[me], local_sem.at[2]),
    )
    for copy in local:
        copy.start()
    barrier = pltpu.get_barrier_semaphore()
    for d in range(5):
        @pl.when(exists[d])
        def _(d=d):
            pl.semaphore_signal(barrier, inc=1, device_id={"blk": target[d]}, device_id_type=MESH)
    pl.semaphore_wait(barrier, sum(e.astype(jnp.int32) for e in exists))
    gram[...] = jnp.zeros_like(gram)
    cross[...] = jnp.zeros_like(cross)
    for copy in local:
        copy.wait()

    def copies(o, d):
        return (
            pltpu.make_async_remote_copy(
                src_ref=buf.at[o], dst_ref=buf.at[o], send_sem=send_sem.at[d, o],
                recv_sem=recv_sem.at[o], device_id={"blk": target[d]}, device_id_type=MESH,
            ),
            pltpu.make_async_remote_copy(
                src_ref=vbuf.at[o], dst_ref=vbuf.at[o], send_sem=vsend_sem.at[d, o],
                recv_sem=vrecv_sem.at[o], device_id={"blk": target[d]}, device_id_type=MESH,
            ),
        )

    def send(cond, o, d):
        @pl.when(cond)
        def _():
            for copy in copies(o, d):
                copy.start()

    def arrive(o):
        for copy in copies(o, 4):
            copy.wait_recv()

    def compute(o):
        p = buf[o, 0].astype(F32)
        t = buf[o, 1].astype(F32)
        v = vbuf[o]
        dd = p - jnp.mean(p, axis=0, keepdims=True)
        db = dd.astype(BF16)
        rb = (t - p).astype(BF16)
        sb = (db.astype(F32) / v).astype(BF16)
        cols = pl.ds(pl.multiple_of(o * width, width), width)
        dev[:, cols] = db
        res[:, cols] = rb
        var_row[:, cols] = v
        gram[...] += lax.dot_general(sb, db, NT, preferred_element_type=F32)
        cross[...] += lax.dot_general(sb, rb, NT, preferred_element_type=F32)

    def lagged(t, lag):
        d = t // 2 - lag
        s = 1 - 2 * (t % 2)
        zo = z - s * d
        valid = (d >= 0) & (zo >= 0) & (zo < nz) & ((d > 0) | (s == 1))
        return d, s, zo, valid

    def step(t, carry):
        d, s, zo, valid = lagged(t, 0)

        @pl.when(valid)
        def _():
            o = (zo * nx + x) * 2 + core

            @pl.when(d > 0)
            def _():
                arrive(o)
            send(((d == 0) | (s == 1)) & exists[0], o, 0)
            send(((d == 0) | (s == -1)) & exists[1], o, 1)
            send(exists[2], o, 2)
            send(exists[3], o, 3)
            send(exists[4], o, 4)
            compute(o)

        _, _, zx, valid_x = lagged(t, 1)

        @pl.when(valid_x)
        def _():
            def over_x(xo, carry):
                @pl.when(xo != x)
                def _():
                    o = (zx * nx + xo) * 2 + core
                    arrive(o)
                    send((xo < x) & exists[2], o, 2)
                    send((xo > x) & exists[3], o, 3)
                    send(exists[4], o, 4)
                    compute(o)
                return carry
            lax.fori_loop(0, nx, over_x, 0)

        _, _, zp, valid_p = lagged(t, 2)

        @pl.when(valid_p)
        def _():
            def over_x(xo, carry):
                o = (zp * nx + xo) * 2 + 1 - core
                arrive(o)
                compute(o)
                return carry
            lax.fori_loop(0, nx, over_x, 0)
        return carry

    lax.fori_loop(0, 2 * (nz + 2), step, 0)

    def drain(k, carry):
        zo = k // nx
        xo = k % nx
        o = k * 2 + core
        sent = (
            (xo == x) & (zo <= z) & exists[0],
            (xo == x) & (zo >= z) & exists[1],
            (xo <= x) & exists[2],
            (xo >= x) & exists[3],
            exists[4],
        )
        for d in range(5):
            @pl.when(sent[d])
            def _(d=d):
                for copy in copies(o, d):
                    copy.wait_send()
        return carry

    lax.fori_loop(0, nz * nx, drain, 0)


def gather(n, pred, targ, var):
    nz, nx = chip_grid(n)
    members, width = pred.shape
    hbm = pl.BlockSpec(memory_space=pl.ANY)
    vmem = pl.BlockSpec(memory_space=pltpu.VMEM)
    sem = pltpu.SemaphoreType.DMA
    return pl.pallas_call(
        functools.partial(gather_kernel, nz, nx),
        out_shape=(
            jax.ShapeDtypeStruct((members, n * width), BF16),
            jax.ShapeDtypeStruct((members, n * width), BF16),
            jax.ShapeDtypeStruct((1, n * width), F32),
            jax.ShapeDtypeStruct((members, members), F32),
            jax.ShapeDtypeStruct((members, members), F32),
        ),
        in_specs=[hbm, hbm, hbm],
        out_specs=(vmem,) * 5,
        scratch_shapes=[
            pltpu.VMEM((n, 2, members, width), BF16),
            pltpu.VMEM((n, 1, width), F32),
            sem((3,)), sem((5, n)), sem((5, n)), sem((n,)), sem((n,)),
        ],
        compiler_params=pltpu.CompilerParams(collective_id=0, has_side_effects=True),
        name="gather_gram",
    )(pred, targ, var)


def rows_of(value, j):
    return jnp.broadcast_to(value[j : j + 1, :], value.shape)


def lanes_of(value, j):
    return jnp.broadcast_to(value[:, j : j + 1], value.shape)


def invert_panel(work, start):
    base = start // 128 * 128
    off = start - base
    other = PANEL - off
    lane = lax.broadcasted_iota(jnp.int32, (8, 128), 1)
    sub = lax.broadcasted_iota(jnp.int32, (8, 128), 0)
    own = (lane >= off) & (lane < off + PANEL)
    groups = []
    for r in range(PANEL // 8):
        block = work[start + 8 * r : start + 8 * r + 8, base : base + 128]
        eye = jnp.where(lane == sub + (other + 8 * r), 1.0, 0.0).astype(F32)
        groups.append(jnp.where(own, block, eye))
    for q in range(PANEL // 8):
        at = off + 8 * q
        rows = groups[q]
        cols = [lanes_of(rows, at + j) for j in range(8)]
        for j in range(8):
            inv = 1.0 / rows_of(cols[j], j)
            here = sub == j
            scaled = rows_of(rows, j) * inv
            rows = jnp.where(here, scaled, rows - cols[j] * scaled)
            for m in range(j + 1, 8):
                scaled = rows_of(cols[m], j) * inv
                cols[m] = jnp.where(here, scaled, cols[m] - cols[j] * scaled)
        final = [rows_of(rows, j) for j in range(8)]
        for r in range(PANEL // 8):
            if r != q:
                parts = [lanes_of(groups[r], at + j) * final[j] for j in range(8)]
                while len(parts) > 1:
                    parts = [parts[i] + parts[i + 1] for i in range(0, len(parts), 2)]
                groups[r] = groups[r] - parts[0]
        groups[q] = rows
    return jnp.concatenate(groups, axis=0)[:, other : other + PANEL]


def solve(gram, cross, work):
    members = gram.shape[0]
    row = lax.broadcasted_iota(jnp.int32, gram.shape, 0)
    col = lax.broadcasted_iota(jnp.int32, gram.shape, 1)
    work[:, :members] = gram[...] + jnp.where(row == col, members - 1.0, 0.0)
    work[:, members:] = cross[...]
    for start in range(0, members, PANEL):
        stop = start + PANEL
        inverse = invert_panel(work, start)
        left = stop // 128 * 128
        panel = jnp.dot(inverse, work[start:stop, left:], precision=HIGHEST, preferred_element_type=F32)
        column = work[:, start:stop]
        update = jnp.dot(column, panel, precision=HIGHEST, preferred_element_type=F32)
        if start:
            work[:start, left:] = work[:start, left:] - update[:start]
        if stop < members:
            work[stop:, left:] = work[stop:, left:] - update[stop:]
        work[start:stop, left:] = panel
    return work[:, members:]


def step_kernel(
    per_step, ids, gram, cross, dev, res, var_row, pair, taper, ens, out, work, vmat, weight
):
    members, data = dev.shape
    slots = ids.shape[0]
    width = data // slots
    tile = members

    @pl.when(pl.program_id(0) == 0)
    def _():
        pairs = pair[...]
        tapers = taper[...]
        for s in range(slots):
            hit = jnp.where(pairs == ids[s], tapers, 0.0)
            total = jnp.sum(hit, axis=1, keepdims=True)
            weight[:, s * width : (s + 1) * width] = jnp.broadcast_to(total, (pairs.shape[0], width))
        xt = jnp.transpose(solve(gram, cross, work))
        high = xt.astype(BF16)
        rest = xt - high.astype(F32)
        mid = rest.astype(BF16)
        low = (rest - mid.astype(F32)).astype(BF16)
        for s in range(0, data, tile):
            cols = slice(s, s + tile)
            d = dev[:, cols]
            update = jnp.dot(low, d, preferred_element_type=F32)
            update += jnp.dot(mid, d, preferred_element_type=F32)
            update += jnp.dot(high, d, preferred_element_type=F32)
            vmat[:, cols] = ((res[:, cols].astype(F32) - update) / var_row[:, cols]).astype(BF16)

    cell = ens.shape[1] // per_step
    for k in range(per_step):
        c = pl.program_id(0) * per_step + k
        u = ens[:, k * cell : (k + 1) * cell].astype(F32)
        u = (u - jnp.mean(u, axis=0, keepdims=True)).astype(BF16)
        scaled = vmat[...] * weight[pl.ds(c, 1), :].astype(BF16)
        total = lax.dot_general(scaled, dev[...], NT, preferred_element_type=F32)
        total = (total * (1.0 / (members - 1.0))).astype(BF16)
        out[:, k * cell : (k + 1) * cell] = jnp.dot(total, u, preferred_element_type=F32)


def finish(ensemble, gram, cross, dev, res, var_row, ids, pair, taper):
    members, cells = ensemble.shape
    blocks = pair.shape[0]
    data = dev.shape[1]
    per_step = 2
    lanes = cells // blocks * per_step
    whole = lambda a: pl.BlockSpec(a.shape, lambda i: (0, 0), pipeline_mode=pl.Buffered(1))
    return pl.pallas_call(
        functools.partial(step_kernel, per_step),
        out_shape=jax.ShapeDtypeStruct((members, cells), F32),
        grid=(blocks // per_step,),
        in_specs=[pl.BlockSpec(memory_space=pltpu.SMEM)]
        + [whole(a) for a in (gram, cross, dev, res, var_row, pair, taper)]
        + [pl.BlockSpec((members, lanes), lambda i: (0, i))],
        out_specs=pl.BlockSpec((members, lanes), lambda i: (0, i)),
        scratch_shapes=[
            pltpu.VMEM((members, 2 * members), F32),
            pltpu.VMEM((members, data), BF16),
            pltpu.VMEM((blocks, data), F32),
        ],
        name="solve_step",
    )(ids, gram, cross, dev, res, var_row, pair, taper, ensemble)


def solution(mesh):
    n = mesh.shape["blk"]

    def per_device(ensemble, predicted, targets, datum_noise_variance, block_ids, pair_blocks, taper):
        dev, res, var_row, gram, cross = gather(
            n, predicted, targets, datum_noise_variance.reshape(1, -1)
        )
        return finish(ensemble, gram, cross, dev, res, var_row, block_ids, pair_blocks, taper)

    in_specs = (
        P(None, ("groups", "blk")),
        P(None, ("groups", "blk")),
        P(None, ("groups", "blk")),
        P(("groups", "blk")),
        P("groups"),
        P(("groups", "blk"), None),
        P(("groups", "blk"), None),
    )
    return jax.shard_map(
        per_device, mesh=mesh, in_specs=in_specs, out_specs=P(None, ("groups", "blk")), check_vma=False
    )
```

```python
import functools

import jax
import jax.numpy as jnp
from jax import lax
from jax.experimental import pallas as pl
from jax.experimental.pallas import tpu as pltpu
from jax.sharding import PartitionSpec as P

MESH = pl.DeviceIdType.MESH
F32 = jnp.float32
BF16 = jnp.bfloat16
HIGHEST = lax.Precision.HIGHEST
NT = (((1,), (1,)), ((), ()))
PANEL = 64
ROWS = 16


def chip_grid(n):
    chips = n // 2
    nx = max(f for f in range(1, chips + 1) if chips % f == 0 and f * f * f <= chips)
    return chips // nx, nx


def gather_kernel(
    nz, nx, pred, targ, var, dev, res, var_row, gram, cross,
    buf, vbuf, local_sem, send_sem, vsend_sem, recv_sem, vrecv_sem,
):
    width = buf.shape[-1]
    me = lax.axis_index("blk")
    core = me % 2
    x = (me // 2) % nx
    z = me // (2 * nx)
    exists = (z < nz - 1, z > 0, x < nx - 1, x > 0, core >= 0)
    target = (me + 2 * nx, me - 2 * nx, me + 2, me - 2, me + 1 - 2 * core)

    local = (
        pltpu.make_async_copy(pred, buf.at[me, 0], local_sem.at[0]),
        pltpu.make_async_copy(targ, buf.at[me, 1], local_sem.at[1]),
        pltpu.make_async_copy(var, vbuf.at[me], local_sem.at[2]),
    )
    for copy in local:
        copy.start()
    barrier = pltpu.get_barrier_semaphore()
    for d in range(5):
        @pl.when(exists[d])
        def _(d=d):
            pl.semaphore_signal(barrier, inc=1, device_id={"blk": target[d]}, device_id_type=MESH)
    pl.semaphore_wait(barrier, sum(e.astype(jnp.int32) for e in exists))
    gram[...] = jnp.zeros_like(gram)
    cross[...] = jnp.zeros_like(cross)
    for copy in local:
        copy.wait()

    def copies(o, d):
        return (
            pltpu.make_async_remote_copy(
                src_ref=buf.at[o], dst_ref=buf.at[o], send_sem=send_sem.at[d, o],
                recv_sem=recv_sem.at[o], device_id={"blk": target[d]}, device_id_type=MESH,
            ),
            pltpu.make_async_remote_copy(
                src_ref=vbuf.at[o], dst_ref=vbuf.at[o], send_sem=vsend_sem.at[d, o],
                recv_sem=vrecv_sem.at[o], device_id={"blk": target[d]}, device_id_type=MESH,
            ),
        )

    def send(cond, o, d):
        @pl.when(cond)
        def _():
            for copy in copies(o, d):
                copy.start()

    def arrive(o):
        for copy in copies(o, 4):
            copy.wait_recv()

    def compute(o):
        p = buf[o, 0].astype(F32)
        t = buf[o, 1].astype(F32)
        v = vbuf[o]
        dd = p - jnp.mean(p, axis=0, keepdims=True)
        db = dd.astype(BF16)
        rb = (t - p).astype(BF16)
        sb = (db.astype(F32) / v).astype(BF16)
        cols = pl.ds(pl.multiple_of(o * width, width), width)
        dev[:, cols] = db
        res[:, cols] = rb
        var_row[:, cols] = v
        gram[...] += lax.dot_general(sb, db, NT, preferred_element_type=F32)
        cross[...] += lax.dot_general(sb, rb, NT, preferred_element_type=F32)

    def lagged(t, lag):
        d = t // 2 - lag
        s = 1 - 2 * (t % 2)
        zo = z - s * d
        valid = (d >= 0) & (zo >= 0) & (zo < nz) & ((d > 0) | (s == 1))
        return d, s, zo, valid

    def step(t, carry):
        d, s, zo, valid = lagged(t, 0)

        @pl.when(valid)
        def _():
            o = (zo * nx + x) * 2 + core

            @pl.when(d > 0)
            def _():
                arrive(o)
            send(((d == 0) | (s == 1)) & exists[0], o, 0)
            send(((d == 0) | (s == -1)) & exists[1], o, 1)
            send(exists[2], o, 2)
            send(exists[3], o, 3)
            send(exists[4], o, 4)

        _, _, zx, valid_x = lagged(t, 1)

        @pl.when(valid_x)
        def _():
            def over_x(xo, carry):
                @pl.when(xo != x)
                def _():
                    o = (zx * nx + xo) * 2 + core
                    arrive(o)
                    send((xo < x) & exists[2], o, 2)
                    send((xo > x) & exists[3], o, 3)
                    send(exists[4], o, 4)
                return carry
            lax.fori_loop(0, nx, over_x, 0)

        @pl.when(valid)
        def _():
            compute((zo * nx + x) * 2 + core)

        @pl.when(valid_x)
        def _():
            def over_x(xo, carry):
                @pl.when(xo != x)
                def _():
                    compute((zx * nx + xo) * 2 + core)
                return carry
            lax.fori_loop(0, nx, over_x, 0)

        _, _, zp, valid_p = lagged(t, 2)

        @pl.when(valid_p)
        def _():
            def over_x(xo, carry):
                o = (zp * nx + xo) * 2 + 1 - core
                arrive(o)
                compute(o)
                return carry
            lax.fori_loop(0, nx, over_x, 0)
        return carry

    lax.fori_loop(0, 2 * (nz + 2), step, 0)

    def drain(k, carry):
        zo = k // nx
        xo = k % nx
        o = k * 2 + core
        sent = (
            (xo == x) & (zo <= z) & exists[0],
            (xo == x) & (zo >= z) & exists[1],
            (xo <= x) & exists[2],
            (xo >= x) & exists[3],
            exists[4],
        )
        for d in range(5):
            @pl.when(sent[d])
            def _(d=d):
                for copy in copies(o, d):
                    copy.wait_send()
        return carry

    lax.fori_loop(0, nz * nx, drain, 0)


def gather(n, pred, targ, var):
    nz, nx = chip_grid(n)
    members, width = pred.shape
    hbm = pl.BlockSpec(memory_space=pl.ANY)
    vmem = pl.BlockSpec(memory_space=pltpu.VMEM)
    sem = pltpu.SemaphoreType.DMA
    return pl.pallas_call(
        functools.partial(gather_kernel, nz, nx),
        out_shape=(
            jax.ShapeDtypeStruct((members, n * width), BF16),
            jax.ShapeDtypeStruct((members, n * width), BF16),
            jax.ShapeDtypeStruct((1, n * width), F32),
            jax.ShapeDtypeStruct((members, members), F32),
            jax.ShapeDtypeStruct((members, members), F32),
        ),
        in_specs=[hbm, hbm, hbm],
        out_specs=(vmem,) * 5,
        scratch_shapes=[
            pltpu.VMEM((n, 2, members, width), BF16),
            pltpu.VMEM((n, 1, width), F32),
            sem((3,)), sem((5, n)), sem((5, n)), sem((n,)), sem((n,)),
        ],
        compiler_params=pltpu.CompilerParams(collective_id=0, has_side_effects=True),
        name="gather_gram",
    )(pred, targ, var)


def rows_of(value, j):
    return jnp.broadcast_to(value[j : j + 1, :], value.shape)


def lanes_of(value, j):
    return jnp.broadcast_to(value[:, j : j + 1], value.shape)


def invert_panel(work, start):
    base = start // 128 * 128
    off = start - base
    other = PANEL - off
    lane = lax.broadcasted_iota(jnp.int32, (8, 128), 1)
    sub = lax.broadcasted_iota(jnp.int32, (8, 128), 0)
    own = (lane >= off) & (lane < off + PANEL)
    groups = []
    for r in range(PANEL // 8):
        block = work[start + 8 * r : start + 8 * r + 8, base : base + 128]
        eye = jnp.where(lane == sub + (other + 8 * r), 1.0, 0.0).astype(F32)
        groups.append(jnp.where(own, block, eye))
    for q in range(PANEL // 8):
        at = off + 8 * q
        rows = groups[q]
        cols = [lanes_of(rows, at + j) for j in range(8)]
        for j in range(8):
            inv = 1.0 / rows_of(cols[j], j)
            here = sub == j
            scaled = rows_of(rows, j) * inv
            rows = jnp.where(here, scaled, rows - cols[j] * scaled)
            for m in range(j + 1, 8):
                scaled = rows_of(cols[m], j) * inv
                cols[m] = jnp.where(here, scaled, cols[m] - cols[j] * scaled)
        final = [rows_of(rows, j) for j in range(8)]
        for r in range(PANEL // 8):
            if r != q:
                parts = [lanes_of(groups[r], at + j) * final[j] for j in range(8)]
                while len(parts) > 1:
                    parts = [parts[i] + parts[i + 1] for i in range(0, len(parts), 2)]
                groups[r] = groups[r] - parts[0]
        groups[q] = rows
    return jnp.concatenate(groups, axis=0)[:, other : other + PANEL]


def solve(gram, cross, work):
    members = gram.shape[0]
    row = lax.broadcasted_iota(jnp.int32, gram.shape, 0)
    col = lax.broadcasted_iota(jnp.int32, gram.shape, 1)
    work[:, :members] = gram[...] + jnp.where(row == col, members - 1.0, 0.0)
    work[:, members:] = cross[...]
    for start in range(0, members, PANEL):
        stop = start + PANEL
        inverse = invert_panel(work, start)
        left = stop // 128 * 128
        panel = jnp.dot(inverse, work[start:stop, left:], precision=HIGHEST, preferred_element_type=F32)
        column = work[:, start:stop]
        update = jnp.dot(column, panel, precision=HIGHEST, preferred_element_type=F32)
        if start:
            work[:start, left:] = work[:start, left:] - update[:start]
        if stop < members:
            work[stop:, left:] = work[stop:, left:] - update[stop:]
        work[start:stop, left:] = panel
    return work[:, members:]


def step_kernel(
    per_step, ids, gram, cross, dev, res, var_row, pair, taper, ens, out, work, gains, mixer, gain_sum
):
    members, data = dev.shape
    slots = ids.shape[0]
    blocks = pair.shape[0]
    width = data // slots

    @pl.when(pl.program_id(0) == 0)
    def _():
        pairs = pair[...]
        tapers = taper[...]
        spread = ROWS * slots
        lane = lax.broadcasted_iota(jnp.int32, (blocks, spread), 1)
        weight = jnp.zeros((blocks, spread), F32)
        for s in range(slots):
            hit = jnp.where(pairs == ids[s], tapers, 0.0)
            total = jnp.sum(hit, axis=1, keepdims=True)
            weight = jnp.where(lane // ROWS == s, total, weight)
        sub = lax.broadcasted_iota(jnp.int32, (ROWS, spread), 0)
        place = lax.broadcasted_iota(jnp.int32, (ROWS, spread), 1) % ROWS == sub
        for c in range(blocks):
            row = jnp.broadcast_to(weight[c : c + 1, :], (ROWS, spread))
            mixer[c * ROWS : (c + 1) * ROWS, :] = jnp.where(place, row, 0.0).astype(BF16)
        xt = jnp.transpose(solve(gram, cross, work))
        high = xt.astype(BF16)
        rest = xt - high.astype(F32)
        mid = rest.astype(BF16)
        low = (rest - mid.astype(F32)).astype(BF16)
        for s in range(slots):
            cols = slice(s * width, (s + 1) * width)
            d = dev[:, cols]
            update = jnp.dot(low, d, preferred_element_type=F32)
            update += jnp.dot(mid, d, preferred_element_type=F32)
            update += jnp.dot(high, d, preferred_element_type=F32)
            v = ((res[:, cols].astype(F32) - update) / var_row[:, cols]).astype(BF16)
            gain = lax.dot_general(v, d, NT, preferred_element_type=F32)
            gains[s] = (gain * (1.0 / (members - 1.0))).astype(BF16)
        mix = mixer[...]
        for j in range(0, members, ROWS):
            stack = gains[:, j : j + ROWS, :].reshape(slots * ROWS, members)
            mixed = jnp.dot(mix, stack, preferred_element_type=F32).astype(BF16)
            gain_sum[:, j : j + ROWS, :] = mixed.reshape(blocks, ROWS, members)

    cell = ens.shape[1] // per_step
    for k in range(per_step):
        c = pl.program_id(0) * per_step + k
        u = ens[:, k * cell : (k + 1) * cell].astype(F32)
        u = (u - jnp.mean(u, axis=0, keepdims=True)).astype(BF16)
        out[:, k * cell : (k + 1) * cell] = jnp.dot(gain_sum[c], u, preferred_element_type=F32)


def finish(ensemble, gram, cross, dev, res, var_row, ids, pair, taper):
    members, cells = ensemble.shape
    blocks = pair.shape[0]
    slots = ids.shape[0]
    per_step = 2
    lanes = cells // blocks * per_step
    whole = lambda a: pl.BlockSpec(a.shape, lambda i: (0, 0), pipeline_mode=pl.Buffered(1))
    return pl.pallas_call(
        functools.partial(step_kernel, per_step),
        out_shape=jax.ShapeDtypeStruct((members, cells), F32),
        grid=(blocks // per_step,),
        in_specs=[pl.BlockSpec(memory_space=pltpu.SMEM)]
        + [whole(a) for a in (gram, cross, dev, res, var_row, pair, taper)]
        + [pl.BlockSpec((members, lanes), lambda i: (0, i))],
        out_specs=pl.BlockSpec((members, lanes), lambda i: (0, i)),
        scratch_shapes=[
            pltpu.VMEM((members, 2 * members), F32),
            pltpu.VMEM((slots, members, members), BF16),
            pltpu.VMEM((blocks * ROWS, slots * ROWS), BF16),
            pltpu.VMEM((blocks, members, members), BF16),
        ],
        name="solve_step",
    )(ids, gram, cross, dev, res, var_row, pair, taper, ensemble)


def solution(mesh):
    n = mesh.shape["blk"]

    def per_device(ensemble, predicted, targets, datum_noise_variance, block_ids, pair_blocks, taper):
        dev, res, var_row, gram, cross = gather(
            n, predicted, targets, datum_noise_variance.reshape(1, -1)
        )
        return finish(ensemble, gram, cross, dev, res, var_row, block_ids, pair_blocks, taper)

    in_specs = (
        P(None, ("groups", "blk")),
        P(None, ("groups", "blk")),
        P(None, ("groups", "blk")),
        P(("groups", "blk")),
        P("groups"),
        P(("groups", "blk"), None),
        P(("groups", "blk"), None),
    )
    return jax.shard_map(
        per_device, mesh=mesh, in_specs=in_specs, out_specs=P(None, ("groups", "blk")), check_vma=False
    )
```

```python
import functools

import jax
import jax.numpy as jnp
from jax import lax
from jax.experimental import pallas as pl
from jax.experimental.pallas import tpu as pltpu
from jax.sharding import PartitionSpec as P

MESH = pl.DeviceIdType.MESH
F32 = jnp.float32
BF16 = jnp.bfloat16
HIGHEST = lax.Precision.HIGHEST
NT = (((1,), (1,)), ((), ()))
PANEL = 64
ROWS = 16


def chip_grid(n):
    chips = n // 2
    nx = max(f for f in range(1, chips + 1) if chips % f == 0 and f * f * f <= chips)
    return chips // nx, nx


def gather_kernel(
    nz, nx, pred, targ, var, dev, res, var_row, gram, cross,
    buf, vbuf, local_sem, send_sem, vsend_sem, recv_sem, vrecv_sem,
):
    width = buf.shape[-1]
    me = lax.axis_index("blk")
    core = me % 2
    x = (me // 2) % nx
    z = me // (2 * nx)
    exists = (z < nz - 1, z > 0, x < nx - 1, x > 0, core >= 0)
    target = (me + 2 * nx, me - 2 * nx, me + 2, me - 2, me + 1 - 2 * core)

    local = (
        pltpu.make_async_copy(pred, buf.at[me, 0], local_sem.at[0]),
        pltpu.make_async_copy(targ, buf.at[me, 1], local_sem.at[1]),
        pltpu.make_async_copy(var, vbuf.at[me], local_sem.at[2]),
    )
    for copy in local:
        copy.start()
    barrier = pltpu.get_barrier_semaphore()
    for d in range(5):
        @pl.when(exists[d])
        def _(d=d):
            pl.semaphore_signal(barrier, inc=1, device_id={"blk": target[d]}, device_id_type=MESH)
    pl.semaphore_wait(barrier, sum(e.astype(jnp.int32) for e in exists))
    gram[...] = jnp.zeros_like(gram)
    cross[...] = jnp.zeros_like(cross)
    for copy in local:
        copy.wait()

    def copies(o, d):
        return (
            pltpu.make_async_remote_copy(
                src_ref=buf.at[o], dst_ref=buf.at[o], send_sem=send_sem.at[d, o],
                recv_sem=recv_sem.at[o], device_id={"blk": target[d]}, device_id_type=MESH,
            ),
            pltpu.make_async_remote_copy(
                src_ref=vbuf.at[o], dst_ref=vbuf.at[o], send_sem=vsend_sem.at[d, o],
                recv_sem=vrecv_sem.at[o], device_id={"blk": target[d]}, device_id_type=MESH,
            ),
        )

    def send(cond, o, d):
        @pl.when(cond)
        def _():
            for copy in copies(o, d):
                copy.start()

    def arrive(o):
        for copy in copies(o, 4):
            copy.wait_recv()

    def compute(o):
        p = buf[o, 0].astype(F32)
        t = buf[o, 1].astype(F32)
        v = vbuf[o]
        dd = p - jnp.mean(p, axis=0, keepdims=True)
        db = dd.astype(BF16)
        rb = (t - p).astype(BF16)
        sb = (db.astype(F32) / v).astype(BF16)
        cols = pl.ds(pl.multiple_of(o * width, width), width)
        dev[:, cols] = db
        res[:, cols] = rb
        var_row[:, cols] = v
        gram[...] += lax.dot_general(sb, db, NT, preferred_element_type=F32)
        cross[...] += lax.dot_general(sb, rb, NT, preferred_element_type=F32)

    def lagged(t, lag):
        d = t // 2 - lag
        s = 1 - 2 * (t % 2)
        zo = z - s * d
        valid = (d >= 0) & (zo >= 0) & (zo < nz) & ((d > 0) | (s == 1))
        return d, s, zo, valid

    def step(t, carry):
        d, s, zo, valid = lagged(t, 0)

        @pl.when(valid)
        def _():
            o = (zo * nx + x) * 2 + core

            @pl.when(d > 0)
            def _():
                arrive(o)
            send(((d == 0) | (s == 1)) & exists[0], o, 0)
            send(((d == 0) | (s == -1)) & exists[1], o, 1)
            send(exists[2], o, 2)
            send(exists[3], o, 3)
            send(exists[4], o, 4)

        _, _, zx, valid_x = lagged(t, 1)

        @pl.when(valid_x)
        def _():
            def over_x(xo, carry):
                @pl.when(xo != x)
                def _():
                    o = (zx * nx + xo) * 2 + core
                    arrive(o)
                    send((xo < x) & exists[2], o, 2)
                    send((xo > x) & exists[3], o, 3)
                    send(exists[4], o, 4)
                return carry
            lax.fori_loop(0, nx, over_x, 0)

        @pl.when(valid)
        def _():
            compute((zo * nx + x) * 2 + core)

        @pl.when(valid_x)
        def _():
            def over_x(xo, carry):
                @pl.when(xo != x)
                def _():
                    compute((zx * nx + xo) * 2 + core)
                return carry
            lax.fori_loop(0, nx, over_x, 0)

        _, _, zp, valid_p = lagged(t, 2)

        @pl.when(valid_p)
        def _():
            def over_x(xo, carry):
                o = (zp * nx + xo) * 2 + 1 - core
                arrive(o)
                compute(o)
                return carry
            lax.fori_loop(0, nx, over_x, 0)
        return carry

    lax.fori_loop(0, 2 * (nz + 2), step, 0)

    def drain(k, carry):
        zo = k // nx
        xo = k % nx
        o = k * 2 + core
        sent = (
            (xo == x) & (zo <= z) & exists[0],
            (xo == x) & (zo >= z) & exists[1],
            (xo <= x) & exists[2],
            (xo >= x) & exists[3],
            exists[4],
        )
        for d in range(5):
            @pl.when(sent[d])
            def _(d=d):
                for copy in copies(o, d):
                    copy.wait_send()
        return carry

    lax.fori_loop(0, nz * nx, drain, 0)


def gather(n, pred, targ, var):
    nz, nx = chip_grid(n)
    members, width = pred.shape
    hbm = pl.BlockSpec(memory_space=pl.ANY)
    vmem = pl.BlockSpec(memory_space=pltpu.VMEM)
    sem = pltpu.SemaphoreType.DMA
    return pl.pallas_call(
        functools.partial(gather_kernel, nz, nx),
        out_shape=(
            jax.ShapeDtypeStruct((members, n * width), BF16),
            jax.ShapeDtypeStruct((members, n * width), BF16),
            jax.ShapeDtypeStruct((1, n * width), F32),
            jax.ShapeDtypeStruct((members, members), F32),
            jax.ShapeDtypeStruct((members, members), F32),
        ),
        in_specs=[hbm, hbm, hbm],
        out_specs=(vmem,) * 5,
        scratch_shapes=[
            pltpu.VMEM((n, 2, members, width), BF16),
            pltpu.VMEM((n, 1, width), F32),
            sem((3,)), sem((5, n)), sem((5, n)), sem((n,)), sem((n,)),
        ],
        compiler_params=pltpu.CompilerParams(collective_id=0, has_side_effects=True),
        name="gather_gram",
    )(pred, targ, var)


def rows_of(value, j):
    return jnp.broadcast_to(value[j : j + 1, :], value.shape)


def lanes_of(value, j):
    return jnp.broadcast_to(value[:, j : j + 1], value.shape)


def invert_panel(work, start):
    base = start // 128 * 128
    off = start - base
    other = PANEL - off
    lane = lax.broadcasted_iota(jnp.int32, (8, 128), 1)
    sub = lax.broadcasted_iota(jnp.int32, (8, 128), 0)
    own = (lane >= off) & (lane < off + PANEL)
    groups = []
    for r in range(PANEL // 8):
        block = work[start + 8 * r : start + 8 * r + 8, base : base + 128]
        eye = jnp.where(lane == sub + (other + 8 * r), 1.0, 0.0).astype(F32)
        groups.append(jnp.where(own, block, eye))
    for q in range(PANEL // 8):
        at = off + 8 * q
        rows = groups[q]
        cols = [lanes_of(rows, at + j) for j in range(8)]
        for j in range(8):
            inv = 1.0 / rows_of(cols[j], j)
            here = sub == j
            scaled = rows_of(rows, j) * inv
            rows = jnp.where(here, scaled, rows - cols[j] * scaled)
            for m in range(j + 1, 8):
                scaled = rows_of(cols[m], j) * inv
                cols[m] = jnp.where(here, scaled, cols[m] - cols[j] * scaled)
        final = [rows_of(rows, j) for j in range(8)]
        for r in range(PANEL // 8):
            if r != q:
                parts = [lanes_of(groups[r], at + j) * final[j] for j in range(8)]
                while len(parts) > 1:
                    parts = [parts[i] + parts[i + 1] for i in range(0, len(parts), 2)]
                groups[r] = groups[r] - parts[0]
        groups[q] = rows
    return jnp.concatenate(groups, axis=0)[:, other : other + PANEL]


def solve(gram, cross, work):
    members = gram.shape[0]
    row = lax.broadcasted_iota(jnp.int32, gram.shape, 0)
    col = lax.broadcasted_iota(jnp.int32, gram.shape, 1)
    work[:, :members] = gram[...] + jnp.where(row == col, members - 1.0, 0.0)
    work[:, members:] = cross[...]
    for start in range(0, members, PANEL):
        stop = start + PANEL
        inverse = invert_panel(work, start)
        left = stop // 128 * 128
        panel = jnp.dot(inverse, work[start:stop, left:], precision=HIGHEST, preferred_element_type=F32)
        column = work[:, start:stop]
        update = jnp.dot(column, panel, precision=HIGHEST, preferred_element_type=F32)
        if start:
            work[:start, left:] = work[:start, left:] - update[:start]
        if stop < members:
            work[stop:, left:] = work[stop:, left:] - update[stop:]
        work[start:stop, left:] = panel
    return work[:, members:]


def step_kernel(
    per_step, ids, gram, cross, dev, res, var_row, pair, taper, ens, out, work, gains, mixer, gain_sum
):
    members, data = dev.shape
    slots = ids.shape[0]
    blocks = pair.shape[0]
    width = data // slots

    @pl.when(pl.program_id(0) == 0)
    def _():
        pairs = pair[...]
        tapers = taper[...]
        spread = ROWS * slots
        lane = lax.broadcasted_iota(jnp.int32, (blocks, spread), 1)
        weight = jnp.zeros((blocks, spread), F32)
        for s in range(slots):
            hit = jnp.where(pairs == ids[s], tapers, 0.0)
            total = jnp.sum(hit, axis=1, keepdims=True)
            weight = jnp.where(lane // ROWS == s, total, weight)
        sub = lax.broadcasted_iota(jnp.int32, (ROWS, spread), 0)
        place = lax.broadcasted_iota(jnp.int32, (ROWS, spread), 1) % ROWS == sub
        for c in range(blocks):
            row = jnp.broadcast_to(weight[c : c + 1, :], (ROWS, spread))
            mixer[c * ROWS : (c + 1) * ROWS, :] = jnp.where(place, row, 0.0).astype(BF16)
        xt = jnp.transpose(solve(gram, cross, work))
        high = xt.astype(BF16)
        rest = xt - high.astype(F32)
        mid = rest.astype(BF16)
        low = (rest - mid.astype(F32)).astype(BF16)
        split = jnp.concatenate([high, mid, low], axis=0)
        for s in range(0, data, 2 * width):
            cols = slice(s, s + 2 * width)
            d = dev[:, cols]
            parts = jnp.dot(split, d, preferred_element_type=F32)
            update = parts[:members] + (parts[members : 2 * members] + parts[2 * members :])
            v = ((res[:, cols].astype(F32) - update) / var_row[:, cols]).astype(BF16)
            for k in range(2):
                half = slice(k * width, (k + 1) * width)
                gain = lax.dot_general(v[:, half], d[:, half], NT, preferred_element_type=F32)
                gains[s // width + k] = (gain * (1.0 / (members - 1.0))).astype(BF16)
        mix = mixer[...]
        for j in range(0, members, ROWS):
            stack = gains[:, j : j + ROWS, :].reshape(slots * ROWS, members)
            mixed = jnp.dot(mix, stack, preferred_element_type=F32).astype(BF16)
            gain_sum[:, j : j + ROWS, :] = mixed.reshape(blocks, ROWS, members)

    cell = ens.shape[1] // per_step
    for k in range(per_step):
        c = pl.program_id(0) * per_step + k
        u = ens[:, k * cell : (k + 1) * cell].astype(F32)
        u = (u - jnp.mean(u, axis=0, keepdims=True)).astype(BF16)
        out[:, k * cell : (k + 1) * cell] = jnp.dot(gain_sum[c], u, preferred_element_type=F32)


def finish(ensemble, gram, cross, dev, res, var_row, ids, pair, taper):
    members, cells = ensemble.shape
    blocks = pair.shape[0]
    slots = ids.shape[0]
    per_step = 4
    lanes = cells // blocks * per_step
    whole = lambda a: pl.BlockSpec(a.shape, lambda i: (0, 0), pipeline_mode=pl.Buffered(1))
    return pl.pallas_call(
        functools.partial(step_kernel, per_step),
        out_shape=jax.ShapeDtypeStruct((members, cells), F32),
        grid=(blocks // per_step,),
        in_specs=[pl.BlockSpec(memory_space=pltpu.SMEM)]
        + [whole(a) for a in (gram, cross, dev, res, var_row, pair, taper)]
        + [pl.BlockSpec((members, lanes), lambda i: (0, i))],
        out_specs=pl.BlockSpec((members, lanes), lambda i: (0, i)),
        scratch_shapes=[
            pltpu.VMEM((members, 2 * members), F32),
            pltpu.VMEM((slots, members, members), BF16),
            pltpu.VMEM((blocks * ROWS, slots * ROWS), BF16),
            pltpu.VMEM((blocks, members, members), BF16),
        ],
        name="solve_step",
    )(ids, gram, cross, dev, res, var_row, pair, taper, ensemble)


def solution(mesh):
    n = mesh.shape["blk"]

    def per_device(ensemble, predicted, targets, datum_noise_variance, block_ids, pair_blocks, taper):
        dev, res, var_row, gram, cross = gather(
            n, predicted, targets, datum_noise_variance.reshape(1, -1)
        )
        return finish(ensemble, gram, cross, dev, res, var_row, block_ids, pair_blocks, taper)

    in_specs = (
        P(None, ("groups", "blk")),
        P(None, ("groups", "blk")),
        P(None, ("groups", "blk")),
        P(("groups", "blk")),
        P("groups"),
        P(("groups", "blk"), None),
        P(("groups", "blk"), None),
    )
    return jax.shard_map(
        per_device, mesh=mesh, in_specs=in_specs, out_specs=P(None, ("groups", "blk")), check_vma=False
    )
```

```python
import functools

import jax
import jax.numpy as jnp
from jax import lax
from jax.experimental import pallas as pl
from jax.experimental.pallas import tpu as pltpu
from jax.sharding import PartitionSpec as P

MESH = pl.DeviceIdType.MESH
F32 = jnp.float32
BF16 = jnp.bfloat16
HIGHEST = lax.Precision.HIGHEST
NT = (((1,), (1,)), ((), ()))
PANEL = 64
ROWS = 16


def chip_grid(n):
    chips = n // 2
    nx = max(f for f in range(1, chips + 1) if chips % f == 0 and f * f * f <= chips)
    return chips // nx, nx


def gather_kernel(
    nz, nx, pred, targ, var, dev, res, var_row, gram, cross,
    buf, vbuf, local_sem, send_sem, vsend_sem, recv_sem, vrecv_sem,
):
    width = buf.shape[-1]
    me = lax.axis_index("blk")
    core = me % 2
    x = (me // 2) % nx
    z = me // (2 * nx)
    exists = (z < nz - 1, z > 0, x < nx - 1, x > 0, core >= 0)
    target = (me + 2 * nx, me - 2 * nx, me + 2, me - 2, me + 1 - 2 * core)

    local = (
        pltpu.make_async_copy(pred, buf.at[me, 0], local_sem.at[0]),
        pltpu.make_async_copy(targ, buf.at[me, 1], local_sem.at[1]),
        pltpu.make_async_copy(var, vbuf.at[me], local_sem.at[2]),
    )
    for copy in local:
        copy.start()
    barrier = pltpu.get_barrier_semaphore()
    for d in range(5):
        @pl.when(exists[d])
        def _(d=d):
            pl.semaphore_signal(barrier, inc=1, device_id={"blk": target[d]}, device_id_type=MESH)
    pl.semaphore_wait(barrier, sum(e.astype(jnp.int32) for e in exists))
    gram[...] = jnp.zeros_like(gram)
    cross[...] = jnp.zeros_like(cross)
    for copy in local:
        copy.wait()

    def copies(o, d, h):
        made = [
            pltpu.make_async_remote_copy(
                src_ref=buf.at[o, h], dst_ref=buf.at[o, h], send_sem=send_sem.at[d, h, o],
                recv_sem=recv_sem.at[h, o], device_id={"blk": target[d]}, device_id_type=MESH,
            )
        ]
        if h == 0:
            made.append(
                pltpu.make_async_remote_copy(
                    src_ref=vbuf.at[o], dst_ref=vbuf.at[o], send_sem=vsend_sem.at[d, o],
                    recv_sem=vrecv_sem.at[o], device_id={"blk": target[d]}, device_id_type=MESH,
                )
            )
        return made

    def send(cond, o, d, h):
        @pl.when(cond)
        def _():
            for copy in copies(o, d, h):
                copy.start()

    def arrive(o, h):
        for copy in copies(o, 4, h):
            copy.wait_recv()

    def compute(o):
        p = buf[o, 0].astype(F32)
        t = buf[o, 1].astype(F32)
        v = vbuf[o]
        dd = p - jnp.mean(p, axis=0, keepdims=True)
        db = dd.astype(BF16)
        rb = (t - p).astype(BF16)
        sb = (db.astype(F32) / v).astype(BF16)
        cols = pl.ds(pl.multiple_of(o * width, width), width)
        dev[:, cols] = db
        res[:, cols] = rb
        var_row[:, cols] = v
        gram[...] += lax.dot_general(sb, db, NT, preferred_element_type=F32)
        cross[...] += lax.dot_general(sb, rb, NT, preferred_element_type=F32)

    def lagged(t, lag):
        d = t // 2 - lag
        s = 1 - 2 * (t % 2)
        zo = z - s * d
        valid = (d >= 0) & (zo >= 0) & (zo < nz) & ((d > 0) | (s == 1))
        return d, s, zo, valid

    def step(t, carry):
        d, s, zo, valid = lagged(t, 0)

        @pl.when(valid)
        def _():
            o = (zo * nx + x) * 2 + core

            for h in range(2):
                @pl.when(d > 0)
                def _(h=h):
                    arrive(o, h)
                send(((d == 0) | (s == 1)) & exists[0], o, 0, h)
                send(((d == 0) | (s == -1)) & exists[1], o, 1, h)
                send(exists[2], o, 2, h)
                send(exists[3], o, 3, h)
                send(exists[4], o, 4, h)

        _, _, zx, valid_x = lagged(t, 1)

        @pl.when(valid_x)
        def _():
            def over_x(xo, carry):
                @pl.when(xo != x)
                def _():
                    o = (zx * nx + xo) * 2 + core
                    for h in range(2):
                        arrive(o, h)
                        send((xo < x) & exists[2], o, 2, h)
                        send((xo > x) & exists[3], o, 3, h)
                        send(exists[4], o, 4, h)
                return carry
            lax.fori_loop(0, nx, over_x, 0)

        @pl.when(valid)
        def _():
            compute((zo * nx + x) * 2 + core)

        @pl.when(valid_x)
        def _():
            def over_x(xo, carry):
                @pl.when(xo != x)
                def _():
                    compute((zx * nx + xo) * 2 + core)
                return carry
            lax.fori_loop(0, nx, over_x, 0)

        _, _, zp, valid_p = lagged(t, 2)

        @pl.when(valid_p)
        def _():
            def over_x(xo, carry):
                o = (zp * nx + xo) * 2 + 1 - core
                arrive(o, 0)
                arrive(o, 1)
                compute(o)
                return carry
            lax.fori_loop(0, nx, over_x, 0)
        return carry

    lax.fori_loop(0, 2 * (nz + 2), step, 0)

    def drain(k, carry):
        zo = k // nx
        xo = k % nx
        o = k * 2 + core
        sent = (
            (xo == x) & (zo <= z) & exists[0],
            (xo == x) & (zo >= z) & exists[1],
            (xo <= x) & exists[2],
            (xo >= x) & exists[3],
            exists[4],
        )
        for d in range(5):
            @pl.when(sent[d])
            def _(d=d):
                for copy in copies(o, d, 0) + copies(o, d, 1):
                    copy.wait_send()
        return carry

    lax.fori_loop(0, nz * nx, drain, 0)


def gather(n, pred, targ, var):
    nz, nx = chip_grid(n)
    members, width = pred.shape
    hbm = pl.BlockSpec(memory_space=pl.ANY)
    vmem = pl.BlockSpec(memory_space=pltpu.VMEM)
    sem = pltpu.SemaphoreType.DMA
    return pl.pallas_call(
        functools.partial(gather_kernel, nz, nx),
        out_shape=(
            jax.ShapeDtypeStruct((members, n * width), BF16),
            jax.ShapeDtypeStruct((members, n * width), BF16),
            jax.ShapeDtypeStruct((1, n * width), F32),
            jax.ShapeDtypeStruct((members, members), F32),
            jax.ShapeDtypeStruct((members, members), F32),
        ),
        in_specs=[hbm, hbm, hbm],
        out_specs=(vmem,) * 5,
        scratch_shapes=[
            pltpu.VMEM((n, 2, members, width), BF16),
            pltpu.VMEM((n, 1, width), F32),
            sem((3,)), sem((5, 2, n)), sem((5, n)), sem((2, n)), sem((n,)),
        ],
        compiler_params=pltpu.CompilerParams(collective_id=0, has_side_effects=True),
        name="gather_gram",
    )(pred, targ, var)


def rows_of(value, j):
    return jnp.broadcast_to(value[j : j + 1, :], value.shape)


def lanes_of(value, j):
    return jnp.broadcast_to(value[:, j : j + 1], value.shape)


def invert_panel(work, start):
    base = start // 128 * 128
    off = start - base
    other = PANEL - off
    lane = lax.broadcasted_iota(jnp.int32, (8, 128), 1)
    sub = lax.broadcasted_iota(jnp.int32, (8, 128), 0)
    own = (lane >= off) & (lane < off + PANEL)
    groups = []
    for r in range(PANEL // 8):
        block = work[start + 8 * r : start + 8 * r + 8, base : base + 128]
        eye = jnp.where(lane == sub + (other + 8 * r), 1.0, 0.0).astype(F32)
        groups.append(jnp.where(own, block, eye))
    for q in range(PANEL // 8):
        at = off + 8 * q
        rows = groups[q]
        cols = [lanes_of(rows, at + j) for j in range(8)]
        for j in range(8):
            inv = 1.0 / rows_of(cols[j], j)
            here = sub == j
            scaled = rows_of(rows, j) * inv
            rows = jnp.where(here, scaled, rows - cols[j] * scaled)
            for m in range(j + 1, 8):
                scaled = rows_of(cols[m], j) * inv
                cols[m] = jnp.where(here, scaled, cols[m] - cols[j] * scaled)
        final = [rows_of(rows, j) for j in range(8)]
        for r in range(PANEL // 8):
            if r != q:
                parts = [lanes_of(groups[r], at + j) * final[j] for j in range(8)]
                while len(parts) > 1:
                    parts = [parts[i] + parts[i + 1] for i in range(0, len(parts), 2)]
                groups[r] = groups[r] - parts[0]
        groups[q] = rows
    return jnp.concatenate(groups, axis=0)[:, other : other + PANEL]


def solve(gram, cross, work):
    members = gram.shape[0]
    row = lax.broadcasted_iota(jnp.int32, gram.shape, 0)
    col = lax.broadcasted_iota(jnp.int32, gram.shape, 1)
    work[:, :members] = gram[...] + jnp.where(row == col, members - 1.0, 0.0)
    work[:, members:] = cross[...]
    for start in range(0, members, PANEL):
        stop = start + PANEL
        inverse = invert_panel(work, start)
        left = stop // 128 * 128
        panel = jnp.dot(inverse, work[start:stop, left:], precision=HIGHEST, preferred_element_type=F32)
        column = work[:, start:stop]
        update = jnp.dot(column, panel, precision=HIGHEST, preferred_element_type=F32)
        if start:
            work[:start, left:] = work[:start, left:] - update[:start]
        if stop < members:
            work[stop:, left:] = work[stop:, left:] - update[stop:]
        work[start:stop, left:] = panel
    return work[:, members:]


def step_kernel(
    per_step, ids, gram, cross, dev, res, var_row, pair, taper, ens, out, work, gains, mixer, gain_sum
):
    members, data = dev.shape
    slots = ids.shape[0]
    blocks = pair.shape[0]
    width = data // slots

    @pl.when(pl.program_id(0) == 0)
    def _():
        pairs = pair[...]
        tapers = taper[...]
        spread = ROWS * slots
        lane = lax.broadcasted_iota(jnp.int32, (blocks, spread), 1)
        weight = jnp.zeros((blocks, spread), F32)
        for s in range(slots):
            hit = jnp.where(pairs == ids[s], tapers, 0.0)
            total = jnp.sum(hit, axis=1, keepdims=True)
            weight = jnp.where(lane // ROWS == s, total, weight)
        sub = lax.broadcasted_iota(jnp.int32, (ROWS, spread), 0)
        place = lax.broadcasted_iota(jnp.int32, (ROWS, spread), 1) % ROWS == sub
        for c in range(blocks):
            row = jnp.broadcast_to(weight[c : c + 1, :], (ROWS, spread))
            mixer[c * ROWS : (c + 1) * ROWS, :] = jnp.where(place, row, 0.0).astype(BF16)
        xt = jnp.transpose(solve(gram, cross, work))
        high = xt.astype(BF16)
        rest = xt - high.astype(F32)
        mid = rest.astype(BF16)
        low = (rest - mid.astype(F32)).astype(BF16)
        split = jnp.concatenate([high, mid, low], axis=0)
        for s in range(0, data, 2 * width):
            cols = slice(s, s + 2 * width)
            d = dev[:, cols]
            parts = jnp.dot(split, d, preferred_element_type=F32)
            update = parts[:members] + (parts[members : 2 * members] + parts[2 * members :])
            v = ((res[:, cols].astype(F32) - update) / var_row[:, cols]).astype(BF16)
            for k in range(2):
                half = slice(k * width, (k + 1) * width)
                gain = lax.dot_general(v[:, half], d[:, half], NT, preferred_element_type=F32)
                gains[s // width + k] = (gain * (1.0 / (members - 1.0))).astype(BF16)
        mix = mixer[...]
        for j in range(0, members, ROWS):
            stack = gains[:, j : j + ROWS, :].reshape(slots * ROWS, members)
            mixed = jnp.dot(mix, stack, preferred_element_type=F32).astype(BF16)
            gain_sum[:, j : j + ROWS, :] = mixed.reshape(blocks, ROWS, members)

    cell = ens.shape[1] // per_step
    for k in range(per_step):
        c = pl.program_id(0) * per_step + k
        u = ens[:, k * cell : (k + 1) * cell].astype(F32)
        u = (u - jnp.mean(u, axis=0, keepdims=True)).astype(BF16)
        out[:, k * cell : (k + 1) * cell] = jnp.dot(gain_sum[c], u, preferred_element_type=F32)


def finish(ensemble, gram, cross, dev, res, var_row, ids, pair, taper):
    members, cells = ensemble.shape
    blocks = pair.shape[0]
    slots = ids.shape[0]
    per_step = 4
    lanes = cells // blocks * per_step
    whole = lambda a: pl.BlockSpec(a.shape, lambda i: (0, 0), pipeline_mode=pl.Buffered(1))
    return pl.pallas_call(
        functools.partial(step_kernel, per_step),
        out_shape=jax.ShapeDtypeStruct((members, cells), F32),
        grid=(blocks // per_step,),
        in_specs=[pl.BlockSpec(memory_space=pltpu.SMEM)]
        + [whole(a) for a in (gram, cross, dev, res, var_row, pair, taper)]
        + [pl.BlockSpec((members, lanes), lambda i: (0, i))],
        out_specs=pl.BlockSpec((members, lanes), lambda i: (0, i)),
        scratch_shapes=[
            pltpu.VMEM((members, 2 * members), F32),
            pltpu.VMEM((slots, members, members), BF16),
            pltpu.VMEM((blocks * ROWS, slots * ROWS), BF16),
            pltpu.VMEM((blocks, members, members), BF16),
        ],
        name="solve_step",
    )(ids, gram, cross, dev, res, var_row, pair, taper, ensemble)


def solution(mesh):
    n = mesh.shape["blk"]

    def per_device(ensemble, predicted, targets, datum_noise_variance, block_ids, pair_blocks, taper):
        dev, res, var_row, gram, cross = gather(
            n, predicted, targets, datum_noise_variance.reshape(1, -1)
        )
        return finish(ensemble, gram, cross, dev, res, var_row, block_ids, pair_blocks, taper)

    in_specs = (
        P(None, ("groups", "blk")),
        P(None, ("groups", "blk")),
        P(None, ("groups", "blk")),
        P(("groups", "blk")),
        P("groups"),
        P(("groups", "blk"), None),
        P(("groups", "blk"), None),
    )
    return jax.shard_map(
        per_device, mesh=mesh, in_specs=in_specs, out_specs=P(None, ("groups", "blk")), check_vma=False
    )
```
